256 devices in a mesh: fsdp: 16 (over y, z_hi), seq: 16 (over x, z_lo, core).
Axes of the slice: x: 4, y: 4, z: 8 (z_hi: 4, z_lo: 2; z = z_hi * 2 + z_lo), core: 2. Of those that a mesh axis runs over, the one named last changes fastest.
Arguments:
- hidden: bfloat16 [16, 2048, 5120], P('fsdp', 'seq'), may hold values from -6 to 6
- queries: bfloat16 [16, 2048, 4096], P('fsdp', 'seq'), may hold values from -400 to 400
- key_value_weight: bfloat16 [5120, 2048], P('fsdp'), may hold values from -0.078125 to 0.078125
- doc_lengths: int32 [16, 16], P('fsdp'), may hold values from 1 to 1024, 2048 in all within a row
- resp_lengths: int32 [16, 16], P('fsdp'), may hold values from 1 to 128
Outputs:
- attended: bfloat16 [16, 2048, 4096], P('fsdp', 'seq')
- pooled: float32 [16, 16, 4096], P('fsdp', None, 'seq')
The draws below stay inside these ranges and needn't reach their ends.
Inputs may be any that keep to these rules, and one draw needn't show every extreme that they name: `doc_lengths`: each row holds the lengths of the documents of one packed sequence in order; they sum to 2048 and the longest is exactly 1024.
All inputs are finite; a program needn't handle non-finite values.
Results may differ from the reference program's by a relative error of at most 0.011.
Values may be sent and summed in bfloat16 or wider, within the bound.
No kernel may reach another device: no remote copies, remote signals or barrier semaphores. Data moves between devices by JAX's collectives and lax.ppermute only.
A program may use at most 128 MiB of HBM per device.

```python
import math
import jax
import jax.numpy as jnp
import numpy as np
from jax import lax

MODEL_WIDTH = 5120
HEAD_SIZE = 128
KEY_VALUE_HEADS = 8
QUERY_HEADS = 32
TOK_DEV = 128
BATCH = 16
PACKED_LENGTH = 2048
DOCS = 16
DOC_MAX = 1024


def draw_queries(key, part):
    base = jnp.clip(jax.random.normal(key, (BATCH, PACKED_LENGTH, QUERY_HEADS, HEAD_SIZE), jnp.float32), -6.0, 6.0)
    return base.reshape(BATCH, PACKED_LENGTH, QUERY_HEADS * HEAD_SIZE).astype(jnp.bfloat16)


def plant(entries, stream_key, low, high):
    longest = entries.shape.index(max(entries.shape))
    spots = []
    for shift in (0, 1):
        where = [jax.random.randint(jax.random.fold_in(stream_key, axis), (), 0, length) for axis, length in enumerate(entries.shape)]
        where[longest] = (where[longest] + shift) % entries.shape[longest]
        spots.append(tuple(where))
    return entries.at[spots[0]].set(low).at[spots[1]].set(high)


def shard_levels(own_key, dims, split, least, high):
    factor_of = 1.0
    for axis_at, shards_of in split:
        draws = jax.random.uniform(jax.random.fold_in(jax.random.fold_in(own_key, 6), axis_at), (shards_of,), jnp.float32, least / len(split), high / len(split))
        factor_of = factor_of * jnp.repeat(jnp.exp(draws), dims[axis_at] // shards_of).reshape((-1,) + (1,) * (len(dims) - 1 - axis_at))
    return factor_of


def profile(number_of, total, bound, lean):
    loads = [(1 << 20) // math.isqrt(grade ** lean) + 1 for grade in range(2, number_of + 1)]
    rest, counts = total - bound - (number_of - 1), [1] * (number_of - 1)
    while rest > 0:
        free = [i for i in range(number_of - 1) if counts[i] < bound]
        whole, left = sum([loads[i] for i in free]), rest
        for i in free:
            addition = min(bound - counts[i], max(1, left * loads[i] // whole), rest)
            counts[i] = counts[i] + addition
            rest = rest - addition
    return np.array([bound] + counts)


def uneven(rng, amount, total, most, slope):
    if amount == 2:
        one = jax.random.randint(rng, (), max(1, total - most), min(most, total - 1) + 1)
        return jnp.stack([one, total - one])
    sizes = jnp.asarray(profile(amount, total, most, slope), jnp.int32)
    pairs = (amount - 1) // 2
    donor, taker = sizes[1:1 + 2 * pairs:2], sizes[2:2 + 2 * pairs:2]
    slack = jnp.minimum(donor - 1, most - taker)
    moved = jax.random.randint(jax.random.fold_in(rng, 1), (pairs,), 0, 1 << 20) % (slack + 1)
    sizes = sizes.at[1:1 + 2 * pairs:2].set(donor - moved).at[2:2 + 2 * pairs:2].set(taker + moved)
    return sizes[jax.random.permutation(jax.random.fold_in(rng, 2), amount)]


def noise(stream_key, shape, spread, limit, shards=(), held_as=jnp.bfloat16):
    level = shard_levels(stream_key, shape, shards, -0.22, 0.18) if shards else 1.0
    result = jax.random.normal(stream_key, shape, jnp.float32) * spread * level
    return jnp.minimum(jnp.maximum(result, -limit), limit).astype(held_as)


def setup_inputs(seed: int = 0) -> dict:
    key_list = jax.random.split(jax.random.key(seed), 6)
    return {
        "hidden": noise(key_list[0], (BATCH, PACKED_LENGTH, MODEL_WIDTH), 1.0, 6.0, ((0, 16), (1, 16))),
        "queries": draw_queries(jax.random.fold_in(key_list[5], 71), 0),
        "key_value_weight": noise(key_list[2], (MODEL_WIDTH, 2 * KEY_VALUE_HEADS * HEAD_SIZE), MODEL_WIDTH ** -0.5, 0.078125, ((0, 16),)),
        "doc_lengths": jax.vmap(lambda own: uneven(own, DOCS, PACKED_LENGTH, DOC_MAX, 2))(jax.random.split(key_list[3], BATCH)).reshape((BATCH, DOCS)).astype(jnp.int32),
        "resp_lengths": plant(jax.random.randint(key_list[4], (BATCH, DOCS), 1, TOK_DEV + 1), jax.random.fold_in(key_list[4], 1), 1, TOK_DEV).astype(jnp.int32),
    }


ROPE_BASE = 1000000.0


def token_tables(lengths, wanted, first, count):
    ends = jnp.cumsum(lengths).astype(jnp.int32)
    starts = ends - lengths
    answer = jnp.minimum(wanted, lengths)
    index = first + jnp.arange(count, dtype=jnp.int32)
    inside = (index[:, None] >= starts[None, :]) & (index[:, None] < ends[None, :])
    token_position = jnp.sum(jnp.where(inside, index[:, None] - starts[None, :], 0), axis=1).astype(jnp.int32)
    doc_id = jnp.sum(jnp.where(index[:, None] >= ends[None, :], 1, 0), axis=1).astype(jnp.int32)
    member = jnp.where(inside & (index[:, None] >= (ends - answer)[None, :]), 1, 0).astype(jnp.int32)
    return token_position, doc_id, member, answer


def rotate_pairs(heads, token_position):
    half = heads.shape[-1] // 2
    freq = ROPE_BASE ** (-(jnp.arange(half, dtype=jnp.float32) * 2.0 / heads.shape[-1]))
    angle = token_position.astype(jnp.float32)[:, None] * freq[None, :]
    cosine = jnp.cos(angle)[:, None, :]
    sine = jnp.sin(angle)[:, None, :]
    first = heads[..., :half]
    second = heads[..., half:]
    return jnp.concatenate([first * cosine - second * sine, second * cosine + first * sine], axis=-1)


def one_sequence(hidden_row, single_query, key_value_weight, lengths, wanted):
    token_position, doc_id, member, answer = token_tables(lengths, wanted, jnp.int32(0), PACKED_LENGTH)
    projected_rows = jnp.dot(hidden_row, key_value_weight, preferred_element_type=jnp.float32)
    key_rows = rotate_pairs(projected_rows[:, :KEY_VALUE_HEADS * HEAD_SIZE].reshape(PACKED_LENGTH, KEY_VALUE_HEADS, HEAD_SIZE), token_position).astype(jnp.bfloat16)
    value_rows = projected_rows[:, KEY_VALUE_HEADS * HEAD_SIZE:].reshape(PACKED_LENGTH, KEY_VALUE_HEADS, HEAD_SIZE).astype(jnp.bfloat16)
    query_group = QUERY_HEADS // KEY_VALUE_HEADS
    query_matrix = single_query.reshape(PACKED_LENGTH, KEY_VALUE_HEADS, query_group, HEAD_SIZE)
    block = min(512, PACKED_LENGTH)
    window = min(PACKED_LENGTH, block + DOC_MAX)

    def attend(index):
        qstart = index * block
        kstart = jnp.maximum(qstart + block - window, 0).astype(jnp.int32)
        qblock = lax.dynamic_slice_in_dim(query_matrix, qstart, block, 0).astype(jnp.float32)
        kblock = lax.dynamic_slice_in_dim(key_rows, kstart, window, 0).astype(jnp.float32)
        vblock = lax.dynamic_slice_in_dim(value_rows, kstart, window, 0).astype(jnp.float32)
        qdoc = lax.dynamic_slice_in_dim(doc_id, qstart, block, 0)
        kdoc = lax.dynamic_slice_in_dim(doc_id, kstart, window, 0)
        qplace = qstart + jnp.arange(block, dtype=jnp.int32)
        kplace = kstart + jnp.arange(window, dtype=jnp.int32)
        allowed = (qdoc[:, None] == kdoc[None, :]) & (kplace[None, :] <= qplace[:, None])
        scores = jnp.einsum("qkgd,skd->kgqs", qblock, kblock) * (HEAD_SIZE ** -0.5)
        scores = jnp.where(allowed, scores, -1e30)
        peak = jnp.max(scores, axis=-1, keepdims=True)
        weight = jnp.where(allowed, jnp.exp(scores - peak), 0.0)
        probs = (weight / jnp.sum(weight, axis=-1, keepdims=True)).astype(jnp.bfloat16)
        output = jnp.einsum("kgqs,skd->qkgd", probs.astype(jnp.float32), vblock)
        return output.astype(jnp.bfloat16).reshape(block, QUERY_HEADS * HEAD_SIZE)

    attended = lax.map(attend, jnp.arange(PACKED_LENGTH // block, dtype=jnp.int32)).reshape(PACKED_LENGTH, QUERY_HEADS * HEAD_SIZE)
    sums = jnp.einsum("tr,tc->rc", member.astype(jnp.float32), attended.astype(jnp.float32))
    pooled = sums / answer.astype(jnp.float32)[:, None]
    return attended, pooled


def reference(hidden, queries, key_value_weight, doc_lengths, resp_lengths):
    def per_row(items):
        return one_sequence(items[0], items[1], key_value_weight, items[2], items[3])

    attended, pooled = lax.map(per_row, (hidden, queries, doc_lengths, resp_lengths))
    return attended, pooled
```

```python
import functools

import jax
import jax.numpy as jnp
from jax import lax
from jax.experimental import pallas as pl
from jax.experimental.pallas import tpu as pltpu
from jax.sharding import PartitionSpec as P

HEAD = 128
TOK = 128
WIDTH = 5120
ROWS = 320
HALF = 160
COLS = 512
OCOLS = 1024
DOCS = 16
ROPE_BASE = 1000000.0
NEG = -1e30
LOG2E = 1.4426950408889634
BF = jnp.bfloat16
F32 = jnp.float32
MIB = 1 << 20


def along_x(v, d):
    return lax.ppermute(v, "seq", [(s, (s // 4 + d) % 4 * 4 + s % 4) for s in range(16)])


def across(v, bits):
    return lax.ppermute(v, "seq", [(s, s ^ bits) for s in range(16)])


def along_y(v, d):
    return lax.ppermute(v, "fsdp", [(f, (f // 4 + d) % 4 * 4 + f % 4) for f in range(16)])


def along_z(v, d):
    return lax.ppermute(v, "fsdp", [(f, f // 4 * 4 + (f + d) % 4) for f in range(16)])


def after(v, *others):
    return lax.optimization_barrier((v, *others))[0]


def proj_kernel(parts, n_groups, *refs):
    idx = refs[0]
    hs = refs[1 : 1 + len(parts)]
    refs = refs[1 + len(parts) :]
    mine, theirs = refs[:n_groups], refs[n_groups : 2 * n_groups]
    cos_ref, sin_ref, out_ref, hbuf, wbuf, hsem, wsem = refs[2 * n_groups :]
    core = idx[16]
    copies = []
    for i, (row, height) in enumerate(parts):
        copies.append(pltpu.make_async_copy(hs[i], hbuf.at[pl.ds(row, height)], hsem.at[i]))
    n = 0
    for a, b in zip(mine, theirs):
        for k in range(a.shape[0]):
            f = idx[n]
            copies.append(pltpu.make_async_copy(a.at[k], wbuf.at[f, core], wsem.at[2 * n]))
            copies.append(pltpu.make_async_copy(b.at[k], wbuf.at[f, 1 - core], wsem.at[2 * n + 1]))
            n += 1
    for c in copies:
        c.start()
    for c in copies:
        c.wait()
    h = hbuf[...]
    cos, sin = cos_ref[...], sin_ref[...]
    for half in range(2):
        w = wbuf[:, :, :, half * 256 : half * 256 + 256].reshape(WIDTH, 256)
        p = jnp.dot(h, w, preferred_element_type=F32)
        for k in range(2):
            v = p[:, k * HEAD : (k + 1) * HEAD]
            if half == 0:
                v = v * cos + pltpu.roll(v, 64, 1) * sin
            lo = half * 256 + k * HEAD
            out_ref[:, lo : lo + HEAD] = v.astype(BF)


def project(idx, pieces, groups, cos, sin):
    parts, row = [], 0
    for h in pieces:
        parts.append((row, h.shape[0]))
        row += h.shape[0]
    mine, theirs = [g[0] for g in groups], [g[1] for g in groups]
    any_spec = pl.BlockSpec(memory_space=pl.ANY)
    vm = pl.BlockSpec(memory_space=pltpu.VMEM)
    return pl.pallas_call(
        functools.partial(proj_kernel, tuple(parts), len(groups)),
        out_shape=jax.ShapeDtypeStruct((row, COLS), BF),
        in_specs=[pl.BlockSpec(memory_space=pltpu.SMEM)]
        + [any_spec] * (len(pieces) + 2 * len(groups))
        + [vm, vm],
        out_specs=vm,
        scratch_shapes=[
            pltpu.VMEM((row, WIDTH), BF),
            pltpu.VMEM((16, 2, HALF, COLS), BF),
            pltpu.SemaphoreType.DMA((len(parts),)),
            pltpu.SemaphoreType.DMA((32,)),
        ],
        compiler_params=pltpu.CompilerParams(vmem_limit_bytes=24 * MIB),
        cost_estimate=pl.CostEstimate(
            flops=2 * row * WIDTH * COLS, bytes_accessed=2 * WIDTH * (COLS + row), transcendentals=0
        ),
        name="project",
    )(idx, *pieces, *mine, *theirs, cos, sin)


def attn_kernel(js, *refs):
    n = len(js)
    idx = refs[0]
    q_refs, refs = refs[1 : 1 + n], refs[1 + n :]
    qs_ref, mem_ref, prev_ref = refs[:3]
    kv_in, refs = refs[3:11], refs[11:]
    o_refs, refs = refs[:n], refs[n:]
    pool_ref, kvbuf, sbuf, mx, ls, acc, sem = refs
    copies = []
    for g in range(4):
        p3, p1 = kv_in[2 * g], kv_in[2 * g + 1]
        for i, j in enumerate((0, 1, 3)):
            copies.append(
                pltpu.make_async_copy(
                    p3.at[pl.ds(i * TOK, TOK)], kvbuf.at[idx[g * 4 + j]], sem.at[g * 4 + j]
                )
            )
        copies.append(pltpu.make_async_copy(p1, kvbuf.at[idx[g * 4 + 2]], sem.at[g * 4 + 2]))
    for c in copies:
        c.start()
    for c in copies:
        c.wait()
    row = lax.broadcasted_iota(jnp.int32, (TOK, TOK), 0)
    lane = lax.broadcasted_iota(jnp.int32, (TOK, TOK), 1)
    factor = HEAD ** (-0.5) * LOG2E
    total = prev_ref[...]
    for t, j in enumerate(js):
        lo, hi = idx[16 + j], idx[20 + j]
        first = qs_ref[j] - lane
        last = row - lane + hi * TOK
        for e in range(2):
            mx[e] = jnp.full((4 * TOK, TOK), NEG, F32)
            ls[e] = jnp.zeros((4 * TOK, TOK), F32)
            acc[e] = jnp.zeros((4 * TOK, HEAD), F32)

        def scores(kb, carry, t=t, lo=lo, first=first, last=last):
            base = kb * TOK
            mask = (first <= base) & (last >= base)
            for e in range(2):
                k = kvbuf[kb, :, e * HEAD : (e + 1) * HEAD]
                for g in range(4):
                    h = (e * 4 + g) * HEAD
                    s = lax.dot_general(
                        q_refs[t][:, h : h + HEAD],
                        k,
                        (((1,), (1,)), ((), ())),
                        preferred_element_type=F32,
                    )
                    s = jnp.where(mask, s, NEG)
                    r = slice(g * TOK, (g + 1) * TOK)
                    sbuf[kb - lo, e, r] = s
                    mx[e, r] = jnp.maximum(mx[e, r], s)
            return carry

        lax.fori_loop(lo, hi + 1, scores, 0)
        for e in range(2):
            peak = jnp.max(mx[e], axis=1, keepdims=True) * factor
            mx[e] = jnp.broadcast_to(peak, (4 * TOK, TOK))

        def values(kb, carry, lo=lo):
            for e in range(2):
                v = kvbuf[kb, :, 256 + e * HEAD : 256 + (e + 1) * HEAD]
                p = jnp.exp2(sbuf[kb - lo, e] * factor - mx[e])
                ls[e] = ls[e] + p
                acc[e] = acc[e] + jnp.dot(p.astype(BF), v, preferred_element_type=F32)
            return carry

        lax.fori_loop(lo, hi + 1, values, 0)
        for e in range(2):
            den = jnp.sum(ls[e], axis=1, keepdims=True)
            o = (acc[e] / den).astype(BF)
            for g in range(4):
                h = (e * 4 + g) * HEAD
                o_refs[t][:, h : h + HEAD] = o[g * TOK : (g + 1) * TOK]
        total = total + jnp.dot(mem_ref[j], o_refs[t][...], preferred_element_type=F32)
    pool_ref[...] = total


def attend(js, idx, qs, starts, member, prev, kv):
    n = len(js)
    vm = pl.BlockSpec(memory_space=pltpu.VMEM)
    any_spec = pl.BlockSpec(memory_space=pl.ANY)
    out = pl.pallas_call(
        functools.partial(attn_kernel, js),
        out_shape=[jax.ShapeDtypeStruct((TOK, OCOLS), BF)] * n
        + [jax.ShapeDtypeStruct((DOCS, OCOLS), F32)],
        in_specs=[pl.BlockSpec(memory_space=pltpu.SMEM)] + [vm] * (n + 3) + [any_spec] * 8,
        out_specs=[vm] * (n + 1),
        scratch_shapes=[
            pltpu.VMEM((16, TOK, COLS), BF),
            pltpu.VMEM((9, 2, 4 * TOK, TOK), F32),
            pltpu.VMEM((2, 4 * TOK, TOK), F32),
            pltpu.VMEM((2, 4 * TOK, TOK), F32),
            pltpu.VMEM((2, 4 * TOK, HEAD), F32),
            pltpu.SemaphoreType.DMA((16,)),
        ],
        compiler_params=pltpu.CompilerParams(vmem_limit_bytes=24 * MIB),
        cost_estimate=pl.CostEstimate(
            flops=n * 2 * 2 * 1024 * 700 * 128, bytes_accessed=3 * MIB, transcendentals=n * 700 * 1024
        ),
        name="attend",
    )(idx, *qs, starts, member, prev, *kv)
    return out[:n], out[n]


def assemble_kernel(idx, *refs):
    ins, out_ref = refs[:4], refs[4]
    for d in range(4):
        lo = pl.multiple_of(idx[d] * OCOLS, OCOLS)
        out_ref[0, :, pl.ds(lo, OCOLS)] = ins[d][...]


def assemble(idx, pieces):
    vm = pl.BlockSpec(memory_space=pltpu.VMEM)
    return pl.pallas_call(
        assemble_kernel,
        out_shape=jax.ShapeDtypeStruct((1, TOK, 4 * OCOLS), BF),
        in_specs=[pl.BlockSpec(memory_space=pltpu.SMEM)] + [vm] * 4,
        out_specs=vm,
        compiler_params=pltpu.CompilerParams(vmem_limit_bytes=8 * MIB),
        cost_estimate=pl.CostEstimate(flops=0, bytes_accessed=2 * MIB, transcendentals=0),
        name="assemble",
    )(idx, *pieces)


def on_device(hidden, queries, weight, doc_lengths, resp_lengths):
    seq, fsdp = lax.axis_index("seq"), lax.axis_index("fsdp")
    x, rest, core = seq // 4, seq % 4, seq % 2
    y, zh = fsdp // 4, fsdp % 4
    h, q = hidden[0], queries[0]
    top, bottom = h[: TOK // 2], h[TOK // 2 :]

    keys = lax.dynamic_slice(weight, (core * HALF, x * 256), (HALF, 256))
    vals = lax.dynamic_slice(weight, (core * HALF, OCOLS + x * 256), (HALF, 256))
    own = jnp.concatenate([keys, vals], axis=1)

    top_left = along_x(top, 1)
    bottom_right = along_x(bottom, -1)
    zs = {0: own, 1: along_z(own, 1), 3: along_z(own, -1)}
    pieces = {(0, 0): own}
    for d in (1, 3, 2):
        pieces[(d, 0)] = along_y(own, d)
    zs[2] = along_z(after(own, zs[1], zs[3]), 2)
    for z in (1, 3, 2):
        pieces[(0, z)] = zs[z]
        for d in (1, 3, 2):
            pieces[(d, z)] = along_y(zs[z], d)
    top2, bottom2 = after((top, bottom), top_left, bottom_right)
    bottom_left = along_x(bottom2, 1)
    top_right = along_x(top2, -1)
    top_far = along_x(top_left, 1)
    bottom_far = along_x(bottom_right, -1)

    order1 = [(d, z) for z in (0, 1, 3) for d in range(4)]
    order2 = [(d, 2) for d in range(4)]
    g1 = jnp.stack([pieces[o] for o in order1])
    g2 = jnp.stack([pieces[o] for o in order2])
    groups = ((g1, across(g1, 1)), (g2, across(g2, 1)))
    widx = jnp.stack(
        [((y - d) % 4) * 4 + (zh - z) % 4 for d, z in order1 + order2] + [core]
    ).astype(jnp.int32)

    lengths, wanted = doc_lengths[0], resp_lengths[0]
    ends = jnp.cumsum(lengths)
    starts = ends - lengths
    answer = jnp.minimum(wanted, lengths)
    block = (x + jnp.arange(4, dtype=jnp.int32)) % 4 * 4 + rest
    token = (block[:, None] * TOK + jnp.arange(TOK, dtype=jnp.int32)[None, :])[:, :, None]
    inside = (token >= starts) & (token < ends)
    begin = jnp.sum(jnp.where(inside, starts, 0), axis=2)
    member = jnp.where(inside & (token >= ends - answer), 1.0, 0.0).astype(BF)
    member = jnp.swapaxes(member, 1, 2)
    position = token[:, :, 0] - begin
    freq = ROPE_BASE ** (-(jnp.arange(HEAD // 2, dtype=F32) * 2.0 / HEAD))
    angle = position.astype(F32)[:, :, None] * freq
    cosine, sine = jnp.cos(angle), jnp.sin(angle)
    cosine = jnp.concatenate([cosine, cosine], axis=-1)
    sine = jnp.concatenate([-sine, sine], axis=-1)
    spread = jnp.broadcast_to(begin[:, :, None], (4, TOK, TOK))
    places = jnp.concatenate([(block ^ m) for m in range(4)])
    aidx = jnp.concatenate([places, begin[:, 0] // TOK, block]).astype(jnp.int32)

    near = [0, 1, 3]
    cos3 = jnp.concatenate([cosine[j] for j in near])
    sin3 = jnp.concatenate([sine[j] for j in near])
    kv3 = project(
        widx, [h, top_right, bottom_right, top_left, bottom_left], groups, cos3, sin3
    )
    kv1 = project(widx, [top_far, bottom_far], groups, cosine[2], sine[2])
    kv3_z = across(kv3, 2)
    kv = [
        kv3, kv1,
        across(kv3, 1), across(kv1, 1),
        kv3_z, across(kv1, 2),
        across(kv3_z, 1), across(kv1, 3),
    ]

    qq = after(q, top_far, bottom_far)
    to = lambda d: lax.dynamic_slice(qq, (0, (x + d) % 4 * OCOLS), (TOK, OCOLS))
    qs = {0: to(0), 3: along_x(to(1), 1), 1: along_x(to(3), -1), 2: along_x(to(2), 2)}

    pool = jnp.zeros((DOCS, OCOLS), F32)
    (o2,), pool = attend((2,), aidx, [qs[2]], spread, member, pool, kv)
    r2 = along_x(o2, 2)
    (o1, o3), pool = attend((1, 3), aidx, [qs[1], qs[3]], spread, member, pool, kv)
    r3 = along_x(o1, 1)
    r1 = along_x(o3, -1)
    (o0,), pool = attend((0,), aidx, [qs[0]], spread, member, pool, kv)
    oidx = ((x + jnp.arange(4, dtype=jnp.int32)) % 4).astype(jnp.int32)
    attended = assemble(oidx, [o0, r1, r2, r3])

    share = lambda m: lax.dynamic_slice(pool, (0, (rest ^ m) * 256), (DOCS, 256))
    sums = share(0) + across(share(1), 1) + across(share(2), 2) + across(share(3), 3)
    pooled = sums / answer.astype(F32)[:, None]
    return attended, pooled[None]


def solution(mesh):
    in_specs = (
        P("fsdp", "seq", None),
        P("fsdp", "seq", None),
        P("fsdp", None),
        P("fsdp", None),
        P("fsdp", None),
    )
    out_specs = (P("fsdp", "seq", None), P("fsdp", None, "seq"))
    return jax.shard_map(
        on_device, mesh=mesh, in_specs=in_specs, out_specs=out_specs, check_vma=False
    )
```

```python
import functools

import jax
import jax.numpy as jnp
from jax import lax
from jax.experimental import pallas as pl
from jax.experimental.pallas import tpu as pltpu
from jax.sharding import PartitionSpec as P


HEAD = 128
TOK = 128
WIDTH = 5120
ROWS = 320
HALF = 160
COLS = 512
OCOLS = 1024
DOCS = 16
ROPE_BASE = 1000000.0
NEG = -1e30
LOG2E = 1.4426950408889634
BF = jnp.bfloat16
F32 = jnp.float32
MIB = 1 << 20
CHUNK = 256


def shift(v, axis, d):
    n = lax.axis_size(axis)
    return lax.ppermute(v, axis, [(i, (i + d) % n) for i in range(n)])


def proj_kernel(n, *refs):
    idx, hs, refs = refs[0], refs[1 : 1 + n], refs[1 + n :]
    sets, refs = (refs[:8], refs[8:16]), refs[16:]
    cos_ref, sin_ref, out_ref, wbuf, acc = refs
    core, zh, my_y = idx[0], idx[1], idx[2]
    span = 4 * ROWS
    for d in range(4):
        for m, c in enumerate((core, 1 - core)):
            for r, turn in enumerate((0, 3, 1)):
                wbuf[d, lax.rem(zh + turn, 4), c] = sets[m][d][r]
            wbuf[d, lax.rem(zh + 2, 4), c] = sets[m][4 + d][...]
        start = pl.multiple_of(lax.rem(my_y + 4 - d, 4) * span, HEAD)
        h = jnp.concatenate([ref[:, pl.ds(start, span)] for ref in hs], axis=0)
        p = jnp.dot(h, wbuf[d].reshape(span, COLS), preferred_element_type=F32)
        if d == 0:
            acc[...] = p
        elif d < 3:
            acc[...] = acc[...] + p
    p = acc[...] + p
    cos, sin = cos_ref[...], sin_ref[...]
    for k in range(4):
        v = p[:, k * HEAD : (k + 1) * HEAD]
        if k < 2:
            v = v * cos + pltpu.roll(v, 64, 1) * sin
        out_ref[:, k * HEAD : (k + 1) * HEAD] = v.astype(BF)


def project(idx, pieces, weights, cos, sin):
    row = sum(h.shape[0] for h in pieces)
    vm = pl.BlockSpec(memory_space=pltpu.VMEM)
    return pl.pallas_call(
        functools.partial(proj_kernel, len(pieces)),
        out_shape=jax.ShapeDtypeStruct((row, COLS), BF),
        in_specs=[pl.BlockSpec(memory_space=pltpu.SMEM)] + [vm] * (len(pieces) + 18),
        out_specs=vm,
        scratch_shapes=[
            pltpu.VMEM((4, 4, 2, HALF, COLS), BF),
            pltpu.VMEM((row, COLS), F32),
        ],
        compiler_params=pltpu.CompilerParams(vmem_limit_bytes=21 * MIB),
        cost_estimate=pl.CostEstimate(
            flops=2 * row * WIDTH * COLS, bytes_accessed=18 * MIB, transcendentals=0
        ),
        name="project",
    )(idx, *pieces, *weights, cos, sin)


def attn_kernel(js, *refs):
    n = len(js)
    idx, qs_ref, mem_ref, prev_ref = refs[:4]
    q_refs, kv_in, refs = refs[4 : 4 + n], refs[4 + n : 12 + n], refs[12 + n :]
    o_refs, refs = refs[:n], refs[n:]
    pool_ref, kvbuf, sbuf, mx, ls, acc = refs
    for g in range(4):
        for j in range(4):
            to = pl.ds(pl.multiple_of(idx[g * 4 + j] * TOK, TOK), TOK)
            row = j % 3 * TOK
            kvbuf[to, :] = kv_in[2 * g + j // 3][row : row + TOK, :]
    kvbuf[pl.ds(16 * TOK, TOK), :] = jnp.zeros((TOK, COLS), BF)
    row = lax.broadcasted_iota(jnp.int32, (TOK, CHUNK), 0)
    lane = lax.broadcasted_iota(jnp.int32, (TOK, CHUNK), 1)
    factor = HEAD ** (-0.5) * LOG2E
    total = jnp.zeros((DOCS, OCOLS), F32)
    for t, j in enumerate(js):
        lo, hi = idx[16 + j], idx[20 + j]
        n_chunks = (hi - lo) // 2 + 1
        first = jnp.concatenate([qs_ref[j], qs_ref[j]], axis=1) - lane
        last = row - lane + hi * TOK
        mx[...] = jnp.full((2, 4 * TOK, TOK), NEG, F32)
        ls[...] = jnp.zeros((2, 4 * TOK, TOK), F32)
        acc[...] = jnp.zeros((2, 4 * TOK, HEAD), F32)

        def scores(i, carry, t=t, lo=lo, first=first, last=last):
            base = pl.multiple_of((lo + 2 * i) * TOK, TOK)
            mask = (first <= base) & (last >= base)
            for e in range(2):
                k = kvbuf[pl.ds(base, CHUNK), e * HEAD : (e + 1) * HEAD]
                for g in range(4):
                    h = (e * 4 + g) * HEAD
                    s = lax.dot_general(
                        q_refs[t][:, h : h + HEAD],
                        k,
                        (((1,), (1,)), ((), ())),
                        preferred_element_type=F32,
                    )
                    s = jnp.where(mask, s, NEG)
                    r = slice(g * TOK, (g + 1) * TOK)
                    sbuf[i, e, r] = s
                    m = jnp.maximum(s[:, :TOK], s[:, TOK:])
                    mx[e, r] = jnp.maximum(mx[e, r], m)
            return carry

        lax.fori_loop(0, n_chunks, scores, 0)
        for e in range(2):
            peak = jnp.max(mx[e], axis=1, keepdims=True) * factor
            mx[e] = jnp.broadcast_to(peak, (4 * TOK, TOK))

        def values(i, carry, lo=lo):
            base = pl.multiple_of((lo + 2 * i) * TOK, TOK)
            for e in range(2):
                v = kvbuf[pl.ds(base, CHUNK), 256 + e * HEAD : 256 + (e + 1) * HEAD]
                for g in range(4):
                    r = slice(g * TOK, (g + 1) * TOK)
                    peak = mx[e, r]
                    p0 = jnp.exp2(sbuf[i, e, r, :TOK] * factor - peak)
                    p1 = jnp.exp2(sbuf[i, e, r, TOK:] * factor - peak)
                    ls[e, r] = ls[e, r] + (p0 + p1)
                    p = jnp.concatenate([p0.astype(BF), p1.astype(BF)], axis=1)
                    acc[e, r] = acc[e, r] + jnp.dot(p, v, preferred_element_type=F32)
            return carry

        lax.fori_loop(0, n_chunks, values, 0)
        for e in range(2):
            den = jnp.sum(ls[e], axis=1, keepdims=True)
            o = (acc[e] / den).astype(BF)
            for g in range(4):
                h = (e * 4 + g) * HEAD
                o_refs[t][:, h : h + HEAD] = o[g * TOK : (g + 1) * TOK]
        total = total + jnp.dot(mem_ref[j], o_refs[t][...], preferred_element_type=F32)
    for zc in range(4):
        part = total[:, zc * 256 : zc * 256 + 256]
        pool_ref[zc % 2, zc // 2] = prev_ref[zc % 2, zc // 2] + part


def attend(js, idx, qs, starts, member, prev, kv):
    n = len(js)
    vm = pl.BlockSpec(memory_space=pltpu.VMEM)
    out = pl.pallas_call(
        functools.partial(attn_kernel, js),
        out_shape=[jax.ShapeDtypeStruct((TOK, OCOLS), BF)] * n
        + [jax.ShapeDtypeStruct((2, 2, DOCS, 256), F32)],
        in_specs=[pl.BlockSpec(memory_space=pltpu.SMEM)] + [vm] * (11 + n),
        out_specs=[vm] * (n + 1),
        scratch_shapes=[
            pltpu.VMEM((17 * TOK, COLS), BF),
            pltpu.VMEM((5, 2, 4 * TOK, CHUNK), F32),
            pltpu.VMEM((2, 4 * TOK, TOK), F32),
            pltpu.VMEM((2, 4 * TOK, TOK), F32),
            pltpu.VMEM((2, 4 * TOK, HEAD), F32),
        ],
        compiler_params=pltpu.CompilerParams(vmem_limit_bytes=15 * MIB),
        cost_estimate=pl.CostEstimate(
            flops=n * 2 * 2 * 1024 * 700 * 128, bytes_accessed=n * 12 * MIB, transcendentals=n * 700 * 1024
        ),
        name="attend",
    )(idx, starts, member, prev, *[qs[j] for j in js], *kv)
    return out[:n], out[n]


def assemble_kernel(idx, *refs):
    ins, out_ref = refs[:4], refs[4]
    for d in range(4):
        lo = pl.multiple_of(idx[d] * OCOLS, OCOLS)
        out_ref[0, :, pl.ds(lo, OCOLS)] = ins[d][...]


def assemble(idx, pieces):
    vm = pl.BlockSpec(memory_space=pltpu.VMEM)
    return pl.pallas_call(
        assemble_kernel,
        out_shape=jax.ShapeDtypeStruct((1, TOK, 4 * OCOLS), BF),
        in_specs=[pl.BlockSpec(memory_space=pltpu.SMEM)] + [vm] * 4,
        out_specs=vm,
        compiler_params=pltpu.CompilerParams(vmem_limit_bytes=4 * MIB),
        cost_estimate=pl.CostEstimate(flops=0, bytes_accessed=2 * MIB, transcendentals=0),
        name="assemble",
    )(idx, *pieces)


def program(hidden, queries, weight, doc_lengths, resp_lengths):
    x, zl, core = lax.axis_index("x"), lax.axis_index("zl"), lax.axis_index("c")
    zh, rest = lax.axis_index("zh"), 2 * zl + core
    h, q = hidden[0], queries[0]

    keys = lax.dynamic_slice(weight, (core * HALF, x * 256), (HALF, 256))
    vals = lax.dynamic_slice(weight, (core * HALF, OCOLS + x * 256), (HALF, 256))
    own = jnp.concatenate([keys, vals], axis=1)
    z1 = shift(own, "zh", 1)
    z3 = shift(own, "zh", -1)
    half = TOK // 2
    top, bottom = h[:half], h[half:]
    top_left = shift(top, "x", 1)
    bottom_right = shift(bottom, "x", -1)
    bottom_left = shift(bottom, "x", 1)
    top_right = shift(top, "x", -1)
    far_top = shift(top_left, "x", 1)
    far_bottom = shift(bottom_right, "x", -1)
    z2 = shift(own, "zh", 2)
    three = jnp.stack([own, z1, z3])
    mine = [three] + [None] * 3 + [z2] + [None] * 3
    for d in (1, 3, 2):
        mine[d] = shift(three, "y", d)
    for d in (1, 3, 2):
        mine[4 + d] = shift(z2, "y", d)
    weights = mine + [shift(v, "c", 1) for v in mine]

    give = lambda d: lax.dynamic_slice(q, (0, (x + d) % 4 * OCOLS), (TOK, OCOLS))
    gives = [give(d) for d in range(4)]
    q1 = shift(gives[3], "x", -1)
    q3 = shift(gives[1], "x", 1)
    q2 = shift(gives[2], "x", 2)
    qs = [gives[0], q1, q3, q2]

    lengths, wanted = doc_lengths[0], resp_lengths[0]
    ends = jnp.cumsum(lengths)
    starts = ends - lengths
    answer = jnp.minimum(wanted, lengths)
    turn = (x + jnp.array([0, 1, 3, 2], jnp.int32)) % 4
    block = turn * 4 + rest
    token = (block[:, None] * TOK + jnp.arange(TOK, dtype=jnp.int32)[None, :])[:, :, None]
    inside = (token >= starts) & (token < ends)
    begin = jnp.sum(jnp.where(inside, starts, 0), axis=2)
    member = jnp.where(inside & (token >= ends - answer), 1.0, 0.0).astype(BF)
    member = jnp.swapaxes(member, 1, 2)
    position = token[:, :, 0] - begin
    pair = jnp.arange(HEAD, dtype=jnp.int32) % (HEAD // 2)
    freq = ROPE_BASE ** (-(pair.astype(F32) * 2.0 / HEAD))
    angle = position.reshape(4 * TOK).astype(F32)[:, None] * freq
    cosine = jnp.cos(angle)
    sine = jnp.where(jnp.arange(HEAD) < HEAD // 2, -1.0, 1.0) * jnp.sin(angle)
    spread = jnp.broadcast_to(begin[:, :, None], (4, TOK, TOK))
    places = jnp.concatenate([(block ^ m) for m in range(4)])
    aidx = jnp.concatenate([places, begin[:, 0] // TOK, block]).astype(jnp.int32)
    widx = jnp.stack([core, zh, lax.axis_index("y")]).astype(jnp.int32)

    cos0, cos1 = cosine[: 3 * TOK], cosine[3 * TOK :]
    sin0, sin1 = sine[: 3 * TOK], sine[3 * TOK :]
    near = [h, top_right, bottom_right, top_left, bottom_left]
    kv_near = project(widx, near, weights, cos0, sin0)
    kv_near_z = shift(kv_near, "zl", 1)
    kv_far = project(widx, [far_top, far_bottom], weights, cos1, sin1)
    kv_far_z = shift(kv_far, "zl", 1)
    kv = []
    for near, far in ((kv_near, kv_far), (kv_near_z, kv_far_z)):
        kv.append([near, far, shift(near, "c", 1), shift(far, "c", 1)])
    kv = kv[0] + kv[1]

    pool = jnp.zeros((2, 2, DOCS, 256), F32)
    (o3,), pool = attend((3,), aidx, qs, spread, member, pool, kv)
    r3 = shift(o3, "x", 2)
    (o1, o2), pool = attend((1, 2), aidx, qs, spread, member, pool, kv)
    r2 = shift(o1, "x", 1)
    r1 = shift(o2, "x", -1)
    (o0,), pool = attend((0,), aidx, qs, spread, member, pool, kv)
    attended = assemble(turn.astype(jnp.int32), [o0, r1, r2, r3])

    pick = lambda v, i: lax.dynamic_index_in_dim(v, i, 0, keepdims=False)
    sums = pick(pool, core) + shift(pick(pool, 1 - core), "c", 1)
    sums = pick(sums, zl) + shift(pick(sums, 1 - zl), "zl", 1)
    pooled = sums / answer.astype(F32)[:, None]
    return attended, pooled[None]


def solution(mesh):
    fine = jax.sharding.Mesh(mesh.devices.reshape(4, 4, 4, 2, 2), ("y", "zh", "x", "zl", "c"))
    fsdp, seq = ("y", "zh"), ("x", "zl", "c")
    in_specs = (
        P(fsdp, seq, None),
        P(fsdp, seq, None),
        P(fsdp, None),
        P(fsdp, None),
        P(fsdp, None),
    )
    out_specs = (P(fsdp, seq, None), P(fsdp, None, seq))
    return jax.shard_map(
        program, mesh=fine, in_specs=in_specs, out_specs=out_specs, check_vma=False
    )
```

```python
import functools

import jax
import jax.numpy as jnp
import numpy as np
from jax import lax
from jax.experimental import pallas as pl
from jax.experimental.pallas import tpu as pltpu
from jax.sharding import PartitionSpec as P


HEAD = 128
TOK = 128
WIDTH = 5120
ROWS = 320
HALF = 160
COLS = 512
OCOLS = 1024
DOCS = 16
ROPE_BASE = 1000000.0
NEG = -1e30
LOG2E = 1.4426950408889634
BF = jnp.bfloat16
F32 = jnp.float32
MIB = 1 << 20
CHUNK = 256


VM = pl.BlockSpec(memory_space=pltpu.VMEM)
SM = pl.BlockSpec(memory_space=pltpu.SMEM)


def shift(v, axis, d):
    n = lax.axis_size(axis)
    return lax.ppermute(v, axis, [(i, (i + d) % n) for i in range(n)])


TURNS = (0, 1, 3, 2)


def block_of(idx, k):
    turn = (idx[0] + TURNS[k]) & 3
    return turn * 4 + idx[1] * 2 + idx[2]


def starts_of(lengths):
    starts = [jnp.int32(0)]
    for r in range(DOCS):
        starts.append(starts[r] + lengths[0, r])
    return starts


def begin_of(token, starts):
    begin = jnp.zeros_like(token)
    for r in range(1, DOCS):
        begin = jnp.where(token >= starts[r], starts[r], begin)
    return begin


def table_kernel(idx, lengths, freq_ref, cos_ref, sin_ref):
    starts = starts_of(lengths)
    row = lax.broadcasted_iota(jnp.int32, (TOK, HEAD), 0)
    lane = lax.broadcasted_iota(jnp.int32, (TOK, HEAD), 1)
    for k in range(4):
        token = row + block_of(idx, k) * TOK
        angle = (token - begin_of(token, starts)).astype(F32) * freq_ref[...]
        rows = slice(k * TOK, (k + 1) * TOK)
        cos_ref[rows, :] = jnp.cos(angle)
        sine = jnp.sin(angle)
        sin_ref[rows, :] = jnp.where(lane < HEAD // 2, -sine, sine)


def tables(idx, lengths, freq):
    out = jax.ShapeDtypeStruct((4 * TOK, HEAD), F32)
    return pl.pallas_call(
        table_kernel,
        out_shape=[out, out],
        in_specs=[SM, SM, VM],
        out_specs=[VM, VM],
        compiler_params=pltpu.CompilerParams(vmem_limit_bytes=4 * MIB),
        cost_estimate=pl.CostEstimate(flops=1 << 22, bytes_accessed=MIB, transcendentals=1 << 17),
        name="tables",
    )(idx, lengths, freq)


def proj_kernel(n, first, *refs):
    idx, hs, refs = refs[0], refs[1 : 1 + n], refs[1 + n :]
    sets, refs = (refs[:8], refs[8:16]), refs[16:]
    cos_ref, sin_ref, out_ref, wbuf, acc = refs
    core, zh, my_y = idx[2], idx[3], idx[4]
    span = 4 * ROWS
    for d in range(4):
        for m, c in enumerate((core, 1 - core)):
            for r, turn in enumerate((0, 3, 1)):
                wbuf[d, lax.rem(zh + turn, 4), c] = sets[m][d][r]
            wbuf[d, lax.rem(zh + 2, 4), c] = sets[m][4 + d][...]
        start = pl.multiple_of(lax.rem(my_y + 4 - d, 4) * span, HEAD)
        h = jnp.concatenate([ref[:, pl.ds(start, span)] for ref in hs], axis=0)
        p = jnp.dot(h, wbuf[d].reshape(span, COLS), preferred_element_type=F32)
        if d == 0:
            acc[...] = p
        elif d < 3:
            acc[...] = acc[...] + p
    p = acc[...] + p
    rows = slice(first, first + p.shape[0])
    cos, sin = cos_ref[rows, :], sin_ref[rows, :]
    for k in range(4):
        v = p[:, k * HEAD : (k + 1) * HEAD]
        if k < 2:
            v = v * cos + pltpu.roll(v, 64, 1) * sin
        out_ref[:, k * HEAD : (k + 1) * HEAD] = v.astype(BF)


def project(idx, first, pieces, weights, cos, sin):
    row = sum(h.shape[0] for h in pieces)
    vm = pl.BlockSpec(memory_space=pltpu.VMEM)
    return pl.pallas_call(
        functools.partial(proj_kernel, len(pieces), first),
        out_shape=jax.ShapeDtypeStruct((row, COLS), BF),
        in_specs=[pl.BlockSpec(memory_space=pltpu.SMEM)] + [vm] * (len(pieces) + 18),
        out_specs=vm,
        scratch_shapes=[
            pltpu.VMEM((4, 4, 2, HALF, COLS), BF),
            pltpu.VMEM((row, COLS), F32),
        ],
        compiler_params=pltpu.CompilerParams(vmem_limit_bytes=21 * MIB),
        cost_estimate=pl.CostEstimate(
            flops=2 * row * WIDTH * COLS, bytes_accessed=18 * MIB, transcendentals=0
        ),
        name="project",
    )(idx, *pieces, *weights, cos, sin)


def attn_kernel(js, *refs):
    n = len(js)
    idx, lengths, wanted, prev_ref = refs[:4]
    q_refs, kv_in, refs = refs[4 : 4 + n], refs[4 + n : 12 + n], refs[12 + n :]
    starts = starts_of(lengths)
    o_refs, refs = refs[:n], refs[n:]
    pool_ref, kvbuf, sbuf, mx, ls, acc = refs
    for g in range(4):
        for j in range(4):
            to = pl.ds(pl.multiple_of((block_of(idx, j) ^ g) * TOK, TOK), TOK)
            row = j % 3 * TOK
            kvbuf[to, :] = kv_in[2 * g + j // 3][row : row + TOK, :]
    kvbuf[pl.ds(16 * TOK, TOK), :] = jnp.zeros((TOK, COLS), BF)
    row = lax.broadcasted_iota(jnp.int32, (TOK, CHUNK), 0)
    lane = lax.broadcasted_iota(jnp.int32, (TOK, CHUNK), 1)
    factor = HEAD ** (-0.5) * LOG2E
    total = jnp.zeros((DOCS, OCOLS), F32)
    for t, j in enumerate(js):
        hi = block_of(idx, j)
        lo = lax.shift_right_logical(begin_of(hi * TOK, starts), 7)
        n_chunks = lax.shift_right_logical(hi - lo, 1) + 1
        begin = begin_of(row[:, :TOK] + hi * TOK, starts)
        first = jnp.concatenate([begin, begin], axis=1) - lane
        last = row - lane + hi * TOK
        mx[...] = jnp.full((2, 4 * TOK, TOK), NEG, F32)
        ls[...] = jnp.zeros((2, 4 * TOK, TOK), F32)
        acc[...] = jnp.zeros((2, 4 * TOK, HEAD), F32)

        def scores(i, carry, t=t, lo=lo, first=first, last=last):
            base = pl.multiple_of((lo + 2 * i) * TOK, TOK)
            mask = (first <= base) & (last >= base)
            for e in range(2):
                k = kvbuf[pl.ds(base, CHUNK), e * HEAD : (e + 1) * HEAD]
                for g in range(4):
                    h = (e * 4 + g) * HEAD
                    s = lax.dot_general(
                        q_refs[t][:, h : h + HEAD],
                        k,
                        (((1,), (1,)), ((), ())),
                        preferred_element_type=F32,
                    )
                    s = jnp.where(mask, s, NEG)
                    r = slice(g * TOK, (g + 1) * TOK)
                    sbuf[i, e, r] = s
                    m = jnp.maximum(s[:, :TOK], s[:, TOK:])
                    mx[e, r] = jnp.maximum(mx[e, r], m)
            return carry

        lax.fori_loop(0, n_chunks, scores, 0)
        for e in range(2):
            peak = jnp.max(mx[e], axis=1, keepdims=True) * factor
            mx[e] = jnp.broadcast_to(peak, (4 * TOK, TOK))

        def values(i, carry, lo=lo):
            base = pl.multiple_of((lo + 2 * i) * TOK, TOK)
            for e in range(2):
                v = kvbuf[pl.ds(base, CHUNK), 256 + e * HEAD : 256 + (e + 1) * HEAD]
                for g in range(4):
                    r = slice(g * TOK, (g + 1) * TOK)
                    peak = mx[e, r]
                    p0 = jnp.exp2(sbuf[i, e, r, :TOK] * factor - peak)
                    p1 = jnp.exp2(sbuf[i, e, r, TOK:] * factor - peak)
                    ls[e, r] = ls[e, r] + (p0 + p1)
                    p = jnp.concatenate([p0.astype(BF), p1.astype(BF)], axis=1)
                    acc[e, r] = acc[e, r] + jnp.dot(p, v, preferred_element_type=F32)
            return carry

        lax.fori_loop(0, n_chunks, values, 0)
        for e in range(2):
            den = jnp.sum(ls[e], axis=1, keepdims=True)
            o = (acc[e] / den).astype(BF)
            for g in range(4):
                h = (e * 4 + g) * HEAD
                o_refs[t][:, h : h + HEAD] = o[g * TOK : (g + 1) * TOK]
        doc = lax.broadcasted_iota(jnp.int32, (DOCS, TOK), 0)
        token = lax.broadcasted_iota(jnp.int32, (DOCS, TOK), 1) + hi * TOK
        member = jnp.zeros((DOCS, TOK), F32)
        for r in range(DOCS):
            answer = jnp.minimum(wanted[0, r], lengths[0, r])
            inside = (token >= starts[r + 1] - answer) & (token < starts[r + 1])
            member = jnp.where((doc == r) & inside, 1.0, member)
        total = total + jnp.dot(member.astype(BF), o_refs[t][...], preferred_element_type=F32)
    for zc in range(4):
        part = total[:, zc * 256 : zc * 256 + 256]
        pool_ref[zc % 2, zc // 2] = prev_ref[zc % 2, zc // 2] + part


def attend(js, idx, lengths, wanted, prev, qs, kv):
    n = len(js)
    vm = pl.BlockSpec(memory_space=pltpu.VMEM)
    out = pl.pallas_call(
        functools.partial(attn_kernel, js),
        out_shape=[jax.ShapeDtypeStruct((TOK, OCOLS), BF)] * n
        + [jax.ShapeDtypeStruct((2, 2, DOCS, 256), F32)],
        in_specs=[SM] * 3 + [vm] * (9 + n),
        out_specs=[vm] * (n + 1),
        scratch_shapes=[
            pltpu.VMEM((17 * TOK, COLS), BF),
            pltpu.VMEM((5, 2, 4 * TOK, CHUNK), F32),
            pltpu.VMEM((2, 4 * TOK, TOK), F32),
            pltpu.VMEM((2, 4 * TOK, TOK), F32),
            pltpu.VMEM((2, 4 * TOK, HEAD), F32),
        ],
        compiler_params=pltpu.CompilerParams(vmem_limit_bytes=15 * MIB),
        cost_estimate=pl.CostEstimate(
            flops=n * 2 * 2 * 1024 * 700 * 128, bytes_accessed=n * 12 * MIB, transcendentals=n * 700 * 1024
        ),
        name="attend",
    )(idx, lengths, wanted, prev, *[qs[j] for j in js], *kv)
    return out[:n], out[n]


def assemble_kernel(idx, *refs):
    ins, out_ref = refs[:4], refs[4]
    for d in range(4):
        lo = pl.multiple_of(((idx[0] + d) & 3) * OCOLS, OCOLS)
        out_ref[0, :, pl.ds(lo, OCOLS)] = ins[d][...]


def assemble(idx, pieces):
    vm = pl.BlockSpec(memory_space=pltpu.VMEM)
    return pl.pallas_call(
        assemble_kernel,
        out_shape=jax.ShapeDtypeStruct((1, TOK, 4 * OCOLS), BF),
        in_specs=[pl.BlockSpec(memory_space=pltpu.SMEM)] + [vm] * 4,
        out_specs=vm,
        compiler_params=pltpu.CompilerParams(vmem_limit_bytes=4 * MIB),
        cost_estimate=pl.CostEstimate(flops=0, bytes_accessed=2 * MIB, transcendentals=0),
        name="assemble",
    )(idx, *pieces)


def program(hidden, queries, weight, doc_lengths, resp_lengths):
    x, zl, core = lax.axis_index("x"), lax.axis_index("zl"), lax.axis_index("c")
    info = jnp.stack([x, zl, core, lax.axis_index("zh"), lax.axis_index("y")]).astype(jnp.int32)
    spots = [((x + d) & 3) * OCOLS for d in range(4)]
    scalars = (x * 256, OCOLS + x * 256, core * HALF, core, 1 - core, zl, 1 - zl, *spots)
    scalars = [v.astype(jnp.uint32) for v in scalars]
    weight, q, info, *scalars = lax.optimization_barrier((weight, queries[0], info, *scalars))
    key_at, value_at, row_at, core, other_core, zl, other_zl, *spots = scalars
    h = hidden[0]

    keys = lax.dynamic_slice(weight, (row_at, key_at), (HALF, 256))
    vals = lax.dynamic_slice(weight, (row_at, value_at), (HALF, 256))
    own = jnp.concatenate([keys, vals], axis=1)
    z1 = shift(own, "zh", 1)
    z3 = shift(own, "zh", -1)
    half = TOK // 2
    top, bottom = h[:half], h[half:]
    top_left = shift(top, "x", 1)
    bottom_right = shift(bottom, "x", -1)
    bottom_left = shift(bottom, "x", 1)
    top_right = shift(top, "x", -1)
    far_top = shift(top_left, "x", 1)
    far_bottom = shift(bottom_right, "x", -1)
    z2 = shift(own, "zh", 2)
    three = jnp.stack([own, z1, z3])
    mine = [three] + [None] * 3 + [z2] + [None] * 3
    for d in (1, 3, 2):
        mine[d] = shift(three, "y", d)
    for d in (1, 3, 2):
        mine[4 + d] = shift(z2, "y", d)
    weights = mine + [shift(v, "c", 1) for v in mine]

    gives = [lax.dynamic_slice(q, (jnp.uint32(0), at), (TOK, OCOLS)) for at in spots]
    q1 = shift(gives[3], "x", -1)
    q3 = shift(gives[1], "x", 1)
    q2 = shift(gives[2], "x", 2)
    qs = [gives[0], q1, q3, q2]

    freq = ROPE_BASE ** (-(np.arange(HEAD) % (HEAD // 2)) * 2.0 / HEAD)
    cosine, sine = tables(info, doc_lengths, jnp.asarray(freq.astype(np.float32)[None]))

    near = [h, top_right, bottom_right, top_left, bottom_left]
    kv_near = project(info, 0, near, weights, cosine, sine)
    kv_near_z = shift(kv_near, "zl", 1)
    kv_far = project(info, 3 * TOK, [far_top, far_bottom], weights, cosine, sine)
    kv_far_z = shift(kv_far, "zl", 1)
    kv = []
    for near, far in ((kv_near, kv_far), (kv_near_z, kv_far_z)):
        kv.append([near, far, shift(near, "c", 1), shift(far, "c", 1)])
    kv = kv[0] + kv[1]

    pool = jnp.zeros((2, 2, DOCS, 256), F32)
    (o3,), pool = attend((3,), info, doc_lengths, resp_lengths, pool, qs, kv)
    r3 = shift(o3, "x", 2)
    (o1, o2), pool = attend((1, 2), info, doc_lengths, resp_lengths, pool, qs, kv)
    r2 = shift(o1, "x", 1)
    r1 = shift(o2, "x", -1)
    (o0,), pool = attend((0,), info, doc_lengths, resp_lengths, pool, qs, kv)
    attended = assemble(info, [o0, r1, r3, r2])

    zero = jnp.uint32(0)
    pick = lambda v, i: lax.dynamic_slice(v, (i,) + (zero,) * (v.ndim - 1), (1, *v.shape[1:]))[0]
    sums = pick(pool, core) + shift(pick(pool, other_core), "c", 1)
    sums = pick(sums, zl) + shift(pick(sums, other_zl), "zl", 1)
    answer = jnp.minimum(resp_lengths[0], doc_lengths[0])
    pooled = sums / answer.astype(F32)[:, None]
    return attended, pooled[None]


def solution(mesh):
    fine = jax.sharding.Mesh(mesh.devices.reshape(4, 4, 4, 2, 2), ("y", "zh", "x", "zl", "c"))
    fsdp, seq = ("y", "zh"), ("x", "zl", "c")
    in_specs = (
        P(fsdp, seq, None),
        P(fsdp, seq, None),
        P(fsdp, None),
        P(fsdp, None),
        P(fsdp, None),
    )
    out_specs = (P(fsdp, seq, None), P(fsdp, None, seq))
    return jax.shard_map(
        program, mesh=fine, in_specs=in_specs, out_specs=out_specs, check_vma=False
    )
```

```python
import functools

import jax
import jax.numpy as jnp
import numpy as np
from jax import lax
from jax.experimental import pallas as pl
from jax.experimental.pallas import tpu as pltpu
from jax.sharding import PartitionSpec as P


HEAD = 128
TOK = 128
WIDTH = 5120
ROWS = 320
HALF = 160
COLS = 512
OCOLS = 1024
DOCS = 16
ROPE_BASE = 1000000.0
NEG = -1e30
LOG2E = 1.4426950408889634
BF = jnp.bfloat16
F32 = jnp.float32
MIB = 1 << 20
CHUNK = 256


VM = pl.BlockSpec(memory_space=pltpu.VMEM)
SM = pl.BlockSpec(memory_space=pltpu.SMEM)


def shift(v, axis, d):
    n = lax.axis_size(axis)
    return lax.ppermute(v, axis, [(i, (i + d) % n) for i in range(n)])


TURNS = (0, 1, 3, 2)


def block_of(idx, k):
    turn = (idx[0] + TURNS[k]) & 3
    return turn * 4 + idx[1] * 2 + idx[2]


def starts_of(lengths):
    starts = [jnp.int32(0)]
    for r in range(DOCS):
        starts.append(starts[r] + lengths[0, r])
    return starts


def begin_of(token, starts):
    begin = jnp.zeros_like(token)
    for r in range(1, DOCS):
        begin = jnp.where(token >= starts[r], starts[r], begin)
    return begin


def table_kernel(idx, lengths, freq_ref, cos_ref, sin_ref):
    starts = starts_of(lengths)
    row = lax.broadcasted_iota(jnp.int32, (TOK, HEAD), 0)
    lane = lax.broadcasted_iota(jnp.int32, (TOK, HEAD), 1)
    for k in range(4):
        token = row + block_of(idx, k) * TOK
        angle = (token - begin_of(token, starts)).astype(F32) * freq_ref[...]
        rows = slice(k * TOK, (k + 1) * TOK)
        cos_ref[rows, :] = jnp.cos(angle)
        sine = jnp.sin(angle)
        sin_ref[rows, :] = jnp.where(lane < HEAD // 2, -sine, sine)


def tables(idx, lengths, freq):
    out = jax.ShapeDtypeStruct((4 * TOK, HEAD), F32)
    return pl.pallas_call(
        table_kernel,
        out_shape=[out, out],
        in_specs=[SM, SM, VM],
        out_specs=[VM, VM],
        compiler_params=pltpu.CompilerParams(vmem_limit_bytes=4 * MIB),
        cost_estimate=pl.CostEstimate(flops=1 << 22, bytes_accessed=MIB, transcendentals=1 << 17),
        name="tables",
    )(idx, lengths, freq)


def proj_kernel(n, first, *refs):
    idx, hs, refs = refs[0], refs[1 : 1 + n], refs[1 + n :]
    sets, refs = (refs[:10], refs[10:20]), refs[20:]
    cos_ref, sin_ref, out_ref, wbuf, acc = refs
    core, zh, my_y = idx[2], idx[3], idx[4]
    span = 4 * ROWS
    for d in range(4):
        for m, c in enumerate((core, 1 - core)):
            for r, turn in enumerate((0, 3, 1, 2)):
                group, part = sets[m][r // 2 * 5 : r // 2 * 5 + 5], r % 2
                piece = group[3 + part][...] if d == 2 else group[(0, 1, 0, 2)[d]][part]
                wbuf[d, lax.rem(zh + turn, 4), c] = piece
        start = pl.multiple_of(lax.rem(my_y + 4 - d, 4) * span, HEAD)
        h = jnp.concatenate([ref[:, pl.ds(start, span)] for ref in hs], axis=0)
        p = jnp.dot(h, wbuf[d].reshape(span, COLS), preferred_element_type=F32)
        if d == 0:
            acc[...] = p
        elif d < 3:
            acc[...] = acc[...] + p
    p = acc[...] + p
    rows = slice(first, first + p.shape[0])
    cos, sin = cos_ref[rows, :], sin_ref[rows, :]
    for k in range(4):
        v = p[:, k * HEAD : (k + 1) * HEAD]
        if k < 2:
            v = v * cos + pltpu.roll(v, 64, 1) * sin
        out_ref[:, k * HEAD : (k + 1) * HEAD] = v.astype(BF)


def project(idx, first, pieces, weights, cos, sin):
    row = sum(h.shape[0] for h in pieces)
    vm = pl.BlockSpec(memory_space=pltpu.VMEM)
    return pl.pallas_call(
        functools.partial(proj_kernel, len(pieces), first),
        out_shape=jax.ShapeDtypeStruct((row, COLS), BF),
        in_specs=[pl.BlockSpec(memory_space=pltpu.SMEM)] + [vm] * (len(pieces) + 22),
        out_specs=vm,
        scratch_shapes=[
            pltpu.VMEM((4, 4, 2, HALF, COLS), BF),
            pltpu.VMEM((row, COLS), F32),
        ],
        compiler_params=pltpu.CompilerParams(vmem_limit_bytes=21 * MIB),
        cost_estimate=pl.CostEstimate(
            flops=2 * row * WIDTH * COLS, bytes_accessed=18 * MIB, transcendentals=0
        ),
        name="project",
    )(idx, *pieces, *weights, cos, sin)


def attn_kernel(js, *refs):
    n = len(js)
    idx, lengths, wanted, prev_ref = refs[:4]
    q_refs, kv_in, refs = refs[4 : 4 + n], refs[4 + n : 12 + n], refs[12 + n :]
    starts = starts_of(lengths)
    o_refs, refs = refs[:n], refs[n:]
    pool_ref, kvbuf, sbuf, mx, ls, acc = refs
    for g in range(4):
        for j in range(4):
            to = pl.ds(pl.multiple_of((block_of(idx, j) ^ g) * TOK, TOK), TOK)
            row = j % 3 * TOK
            kvbuf[to, :] = kv_in[2 * g + j // 3][row : row + TOK, :]
    kvbuf[pl.ds(16 * TOK, TOK), :] = jnp.zeros((TOK, COLS), BF)
    row = lax.broadcasted_iota(jnp.int32, (TOK, CHUNK), 0)
    lane = lax.broadcasted_iota(jnp.int32, (TOK, CHUNK), 1)
    factor = HEAD ** (-0.5) * LOG2E
    total = jnp.zeros((DOCS, OCOLS), F32)
    for t, j in enumerate(js):
        hi = block_of(idx, j)
        lo = lax.shift_right_logical(begin_of(hi * TOK, starts), 7)
        n_chunks = lax.shift_right_logical(hi - lo, 1) + 1
        begin = begin_of(row[:, :TOK] + hi * TOK, starts)
        first = jnp.concatenate([begin, begin], axis=1) - lane
        last = row - lane + hi * TOK
        mx[...] = jnp.full((2, 4 * TOK, TOK), NEG, F32)
        ls[...] = jnp.zeros((2, 4 * TOK, TOK), F32)
        acc[...] = jnp.zeros((2, 4 * TOK, HEAD), F32)

        def scores(i, carry, t=t, lo=lo, first=first, last=last):
            base = pl.multiple_of((lo + 2 * i) * TOK, TOK)
            mask = (first <= base) & (last >= base)
            for e in range(2):
                k = kvbuf[pl.ds(base, CHUNK), e * HEAD : (e + 1) * HEAD]
                for g in range(4):
                    h = (e * 4 + g) * HEAD
                    s = lax.dot_general(
                        q_refs[t][:, h : h + HEAD],
                        k,
                        (((1,), (1,)), ((), ())),
                        preferred_element_type=F32,
                    )
                    s = jnp.where(mask, s, NEG)
                    r = slice(g * TOK, (g + 1) * TOK)
                    sbuf[i, e, r] = s
                    m = jnp.maximum(s[:, :TOK], s[:, TOK:])
                    mx[e, r] = jnp.maximum(mx[e, r], m)
            return carry

        lax.fori_loop(0, n_chunks, scores, 0)
        for e in range(2):
            peak = jnp.max(mx[e], axis=1, keepdims=True) * factor
            mx[e] = jnp.broadcast_to(peak, (4 * TOK, TOK))

        def values(i, carry, lo=lo):
            base = pl.multiple_of((lo + 2 * i) * TOK, TOK)

            def one_head(e, inner):
                v = kvbuf[pl.ds(base, CHUNK), pl.ds(pl.multiple_of(256 + e * HEAD, HEAD), HEAD)]
                for g in range(4):
                    r = slice(g * TOK, (g + 1) * TOK)
                    peak = mx[e, r]
                    p0 = jnp.exp2(sbuf[i, e, r, :TOK] * factor - peak)
                    p1 = jnp.exp2(sbuf[i, e, r, TOK:] * factor - peak)
                    ls[e, r] = ls[e, r] + (p0 + p1)
                    p = jnp.concatenate([p0.astype(BF), p1.astype(BF)], axis=1)
                    acc[e, r] = acc[e, r] + jnp.dot(p, v, preferred_element_type=F32)
                return inner

            return lax.fori_loop(0, 2, one_head, carry)

        lax.fori_loop(0, n_chunks, values, 0)
        for e in range(2):
            den = jnp.sum(ls[e], axis=1, keepdims=True)
            o = (acc[e] / den).astype(BF)
            for g in range(4):
                h = (e * 4 + g) * HEAD
                o_refs[t][:, h : h + HEAD] = o[g * TOK : (g + 1) * TOK]
        doc = lax.broadcasted_iota(jnp.int32, (DOCS, TOK), 0)
        token = lax.broadcasted_iota(jnp.int32, (DOCS, TOK), 1) + hi * TOK
        member = jnp.zeros((DOCS, TOK), F32)
        for r in range(DOCS):
            answer = jnp.minimum(wanted[0, r], lengths[0, r])
            inside = (token >= starts[r + 1] - answer) & (token < starts[r + 1])
            member = jnp.where((doc == r) & inside, 1.0, member)
        total = total + jnp.dot(member.astype(BF), o_refs[t][...], preferred_element_type=F32)
    for zc in range(4):
        part = total[:, zc * 256 : zc * 256 + 256]
        pool_ref[zc % 2, zc // 2] = prev_ref[zc % 2, zc // 2] + part


def attend(js, idx, lengths, wanted, prev, qs, kv):
    n = len(js)
    vm = pl.BlockSpec(memory_space=pltpu.VMEM)
    out = pl.pallas_call(
        functools.partial(attn_kernel, js),
        out_shape=[jax.ShapeDtypeStruct((TOK, OCOLS), BF)] * n
        + [jax.ShapeDtypeStruct((2, 2, DOCS, 256), F32)],
        in_specs=[SM] * 3 + [vm] * (9 + n),
        out_specs=[vm] * (n + 1),
        scratch_shapes=[
            pltpu.VMEM((17 * TOK, COLS), BF),
            pltpu.VMEM((5, 2, 4 * TOK, CHUNK), F32),
            pltpu.VMEM((2, 4 * TOK, TOK), F32),
            pltpu.VMEM((2, 4 * TOK, TOK), F32),
            pltpu.VMEM((2, 4 * TOK, HEAD), F32),
        ],
        compiler_params=pltpu.CompilerParams(vmem_limit_bytes=15 * MIB),
        cost_estimate=pl.CostEstimate(
            flops=n * 2 * 2 * 1024 * 700 * 128, bytes_accessed=n * 12 * MIB, transcendentals=n * 700 * 1024
        ),
        name="attend",
    )(idx, lengths, wanted, prev, *[qs[j] for j in js], *kv)
    return out[:n], out[n]


def assemble_kernel(idx, *refs):
    ins, out_ref = refs[:4], refs[4]
    for d in range(4):
        lo = pl.multiple_of(((idx[0] + d) & 3) * OCOLS, OCOLS)
        out_ref[0, :, pl.ds(lo, OCOLS)] = ins[d][...]


def assemble(idx, pieces):
    vm = pl.BlockSpec(memory_space=pltpu.VMEM)
    return pl.pallas_call(
        assemble_kernel,
        out_shape=jax.ShapeDtypeStruct((1, TOK, 4 * OCOLS), BF),
        in_specs=[pl.BlockSpec(memory_space=pltpu.SMEM)] + [vm] * 4,
        out_specs=vm,
        compiler_params=pltpu.CompilerParams(vmem_limit_bytes=4 * MIB),
        cost_estimate=pl.CostEstimate(flops=0, bytes_accessed=2 * MIB, transcendentals=0),
        name="assemble",
    )(idx, *pieces)


def program(hidden, queries, weight, doc_lengths, resp_lengths):
    x, zl, core = lax.axis_index("x"), lax.axis_index("zl"), lax.axis_index("c")
    info = jnp.stack([x, zl, core, lax.axis_index("zh"), lax.axis_index("y")]).astype(jnp.int32)
    spots = [((x + d) & 3) * OCOLS for d in range(4)]
    scalars = (x * 256, OCOLS + x * 256, core * HALF, core, 1 - core, zl, 1 - zl, *spots)
    scalars = [v.astype(jnp.uint32) for v in scalars]
    weight, q, info, *scalars = lax.optimization_barrier((weight, queries[0], info, *scalars))
    key_at, value_at, row_at, core, other_core, zl, other_zl, *spots = scalars
    h = hidden[0]

    keys = lax.dynamic_slice(weight, (row_at, key_at), (HALF, 256))
    vals = lax.dynamic_slice(weight, (row_at, value_at), (HALF, 256))
    own = jnp.concatenate([keys, vals], axis=1)
    z1 = shift(own, "zh", 1)
    half = TOK // 2
    top, bottom = h[:half], h[half:]
    top_left = shift(top, "x", 1)
    bottom_right = shift(bottom, "x", -1)
    bottom_left = shift(bottom, "x", 1)
    top_right = shift(top, "x", -1)
    far_top = shift(top_left, "x", 1)
    far_bottom = shift(bottom_right, "x", -1)
    z3 = shift(own, "zh", -1)
    z2 = shift(z1, "zh", 1)
    first, last = jnp.stack([own, z1]), jnp.stack([z3, z2])
    mine = []
    for both in (first, last):
        one = shift(both, "y", 1)
        three = shift(both, "y", -1)
        far0 = shift(one[0], "y", 1)
        far1 = shift(three[1], "y", -1)
        mine += [both, one, three, far0, far1]
    theirs = []
    for v in mine:
        theirs.append(shift(v, "c", 1))
    weights = mine + theirs

    gives = [lax.dynamic_slice(q, (jnp.uint32(0), at), (TOK, OCOLS)) for at in spots]
    q1 = shift(gives[3], "x", -1)
    q3 = shift(gives[1], "x", 1)
    q2 = shift(gives[2], "x", 2)
    qs = [gives[0], q1, q3, q2]

    freq = ROPE_BASE ** (-(np.arange(HEAD) % (HEAD // 2)) * 2.0 / HEAD)
    cosine, sine = tables(info, doc_lengths, jnp.asarray(freq.astype(np.float32)[None]))

    near = [h, top_right, bottom_right, top_left, bottom_left]
    kv_near = project(info, 0, near, weights, cosine, sine)
    kv_near_z = shift(kv_near, "zl", 1)
    kv_far = project(info, 3 * TOK, [far_top, far_bottom], weights, cosine, sine)
    kv_far_z = shift(kv_far, "zl", 1)
    kv = []
    for near, far in ((kv_near, kv_far), (kv_near_z, kv_far_z)):
        kv.append([near, far, shift(near, "c", 1), shift(far, "c", 1)])
    kv = kv[0] + kv[1]

    pool = jnp.zeros((2, 2, DOCS, 256), F32)
    (o3,), pool = attend((3,), info, doc_lengths, resp_lengths, pool, qs, kv)
    r3 = shift(o3, "x", 2)
    (o1, o2), pool = attend((1, 2), info, doc_lengths, resp_lengths, pool, qs, kv)
    r2 = shift(o1, "x", 1)
    r1 = shift(o2, "x", -1)
    (o0,), pool = attend((0,), info, doc_lengths, resp_lengths, pool, qs, kv)
    attended = assemble(info, [o0, r1, r3, r2])

    zero = jnp.uint32(0)
    pick = lambda v, i: lax.dynamic_slice(v, (i,) + (zero,) * (v.ndim - 1), (1, *v.shape[1:]))[0]
    sums = pick(pool, core) + shift(pick(pool, other_core), "c", 1)
    sums = pick(sums, zl) + shift(pick(sums, other_zl), "zl", 1)
    answer = jnp.minimum(resp_lengths[0], doc_lengths[0])
    pooled = sums / answer.astype(F32)[:, None]
    return attended, pooled[None]


def solution(mesh):
    fine = jax.sharding.Mesh(mesh.devices.reshape(4, 4, 4, 2, 2), ("y", "zh", "x", "zl", "c"))
    fsdp, seq = ("y", "zh"), ("x", "zl", "c")
    in_specs = (
        P(fsdp, seq, None),
        P(fsdp, seq, None),
        P(fsdp, None),
        P(fsdp, None),
        P(fsdp, None),
    )
    out_specs = (P(fsdp, seq, None), P(fsdp, None, seq))
    return jax.shard_map(
        program, mesh=fine, in_specs=in_specs, out_specs=out_specs, check_vma=False
    )
```
